1024 devices in a mesh: region: 64 (over z, core), mp: 16 (over y, x).
Axes of the slice: x: 4, y: 4, z: 32, core: 2. Of those that a mesh axis runs over, the one named last changes fastest.
Arguments:
- observations: bfloat16 [64, 64, 64, 256], P('region'), may hold values from -8 to 8
- cotangent: bfloat16 [64, 64, 16, 2048], P('region', None, 'mp'), may hold values from -96 to 96
- keys_values: bfloat16 [2, 512, 32768], P(None, 'mp', 'region'), may hold values from -6 to 6
- query_weight: bfloat16 [512, 256], P('mp'), may hold values from -1 to 1
- counts: int32 [64, 64], replicated, may hold values from 0 to 64, as said below
Outputs:
- pair_grad: float32 [2, 512, 32768], P(None, 'mp', 'region')
- projection_grad: float32 [512, 256], P('mp')
The draws below stay inside these ranges and needn't reach their ends.
Inputs may be any that keep to these rules, and one draw needn't show every extreme that they name: counts[s, d] live observations lead block [s, d]; later slots are padding. Every region has a full block from some ingest shard, and some region has full blocks from every ingest shard.
All inputs are finite; a program needn't handle non-finite values.
Results may differ from the reference program's by a relative error of at most 0.008.
The reference program's roundings to bfloat16 on the way (of `queries`, `out_grad`, `reach`, `rounded`, `score_grad` and `query_grad`) count: a program that leaves them out, or rounds other values in their place, can miss the bound.
Values may be sent and summed in bfloat16 or wider, within the bound.
A program may use at most 32 MiB of HBM per device.

```python
import math
import jax
import jax.numpy as jnp
from jax import lax

OBS_WIDTH = 256
HEADS = 16
HEAD_DIM = 32
CAP = 64
LAT = 512
INNER = 512
NODES = 32768
N_REGION = 64


def draw_observations(key, part):
    extent = (N_REGION, N_REGION, CAP, OBS_WIDTH)
    noise_key = jax.random.fold_in(key, 101)
    drawn = jax.random.truncated_normal(noise_key, -6.0, 6.0, extent, jnp.float32)
    return drawn.astype(jnp.bfloat16)


def draw_keys_values(key, part):
    extent = (2, INNER, NODES)
    noise_key = jax.random.fold_in(key, 202)
    drawn = jax.random.truncated_normal(noise_key, -6.0, 6.0, extent, jnp.float32)
    return drawn.astype(jnp.bfloat16)


def draw_query_weight(key, part):
    extent = (INNER, OBS_WIDTH)
    noise_key = jax.random.fold_in(key, 303)
    drawn = jax.random.truncated_normal(noise_key, -5.0, 5.0, extent, jnp.float32) / math.sqrt(OBS_WIDTH)
    return drawn.astype(jnp.bfloat16)


def draw_counts(key, part):
    first_key = jax.random.fold_in(key, 401)
    second_key = jax.random.fold_in(key, 402)
    third_key = jax.random.fold_in(key, 403)
    fourth_key = jax.random.fold_in(key, 404)
    uneven = jax.random.randint(first_key, (N_REGION, N_REGION), 0, CAP + 1)
    region_load = jax.random.randint(second_key, (1, N_REGION), 1, 7)
    uneven = jnp.minimum(uneven * region_load // 4, CAP)
    order = jax.random.permutation(third_key, N_REGION)
    region_index = jnp.arange(N_REGION)
    busiest = jax.random.randint(fourth_key, (), 0, N_REGION)
    filled = (region_index[:, None] == order[None, :]) | (region_index[None, :] == busiest)
    return jnp.where(filled, CAP, uneven).astype(jnp.int32)


def levels(rng, shape, split, smallest, top_value):
    def one(dim, parts):
        heights = jax.random.uniform(jax.random.fold_in(jax.random.fold_in(rng, 6), dim), (parts,), jnp.float32, smallest / len(split), top_value / len(split))
        return jnp.repeat(jnp.exp(heights), shape[dim] // parts).reshape((-1,) + (1,) * (len(shape) - dim - 1))

    gain = one(*split[0])
    for cut in split[1:]:
        gain = gain * one(*cut)
    return gain


def noise(rng, dims, deviation, limit, cuts=(), kind=jnp.bfloat16):
    gain = levels(rng, dims, cuts, -0.22, 0.18) if cuts else 1.0
    result = jax.random.normal(rng, dims, jnp.float32) * deviation * gain
    return jnp.minimum(jnp.maximum(result, -limit), limit).astype(kind)


def setup_inputs(seed: int = 0) -> dict:
    key_of = jax.random.split(jax.random.key(seed), 6)
    observations = draw_observations(jax.random.fold_in(key_of[5], 71), 0)
    cotangent = noise(key_of[1], (N_REGION, N_REGION, HEADS, CAP * HEAD_DIM), 16.0, 96.0, ((0, 64), (2, 16)))
    keys_values = draw_keys_values(jax.random.fold_in(key_of[5], 71), 0)
    query_weight = draw_query_weight(jax.random.fold_in(key_of[5], 71), 0)
    counts = draw_counts(jax.random.fold_in(key_of[5], 71), 0)
    return {"observations": observations, "cotangent": cotangent, "keys_values": keys_values, "query_weight": query_weight, "counts": counts}


def region_grad(items):
    queries, out_grad, reach = items
    scale_back = 1.0 / math.sqrt(HEAD_DIM)
    query_rows = queries.reshape(HEADS, N_REGION * CAP, HEAD_DIM).astype(jnp.float32)
    grad_rows = out_grad.reshape(HEADS, N_REGION * CAP, HEAD_DIM).astype(jnp.float32)
    key_block = reach[0].astype(jnp.float32)
    value_block = reach[1].astype(jnp.float32)
    scores = jnp.einsum('hre,hek->hrk', query_rows, key_block) * scale_back
    row_max = lax.optimization_barrier(jnp.max(scores, axis=2, keepdims=True))
    powers = jnp.exp(scores - row_max)
    attention = powers / lax.optimization_barrier(jnp.sum(powers, axis=2, keepdims=True))
    rounded = lax.optimization_barrier(attention.astype(jnp.bfloat16)).astype(jnp.float32)
    prob_grad = jnp.einsum('hre,hek->hrk', grad_rows, value_block)
    row_dot = lax.optimization_barrier(jnp.sum(attention * prob_grad, axis=2, keepdims=True))
    score_grad = (attention * (prob_grad - row_dot)).astype(jnp.bfloat16)
    score_grad = lax.optimization_barrier(score_grad).astype(jnp.float32)
    query_grad = (jnp.einsum('hrk,hek->hre', score_grad, key_block) * scale_back).astype(jnp.bfloat16)
    key_grad = jnp.einsum('hre,hrk->hek', query_rows, score_grad) * scale_back
    value_grad = jnp.einsum('hre,hrk->hek', grad_rows, rounded)
    return (query_grad, jnp.stack([key_grad, value_grad]))

def reference(observations, cotangent, keys_values, query_weight, counts):
    slot_index = jnp.arange(CAP, dtype=jnp.int32)
    live = slot_index[None, None, :] < counts[:, :, None]
    weight_heads = query_weight.reshape(HEADS, HEAD_DIM, OBS_WIDTH).astype(jnp.float32)
    queries = jnp.einsum('sdcf,hef->dhsce', observations.astype(jnp.float32), weight_heads).astype(jnp.bfloat16)
    out_grad = cotangent.reshape(N_REGION, N_REGION, HEADS, CAP, HEAD_DIM)
    out_grad = jnp.where(live[:, :, None, :, None], out_grad, jnp.zeros((), jnp.bfloat16))
    out_grad = out_grad.transpose(1, 2, 0, 3, 4)
    pairs = keys_values.reshape(2, HEADS, HEAD_DIM, N_REGION, LAT).transpose(3, 0, 1, 2, 4)
    reach = jnp.concatenate([pairs, jnp.roll(pairs, -1, axis=0)], axis=-1)
    query_grad, reach_grad = lax.map(region_grad, (queries, out_grad, reach))
    own = reach_grad[..., :LAT] + jnp.roll(reach_grad[..., LAT:], 1, axis=0)
    pair_grad = own.transpose(1, 2, 3, 0, 4).reshape(2, HEADS * HEAD_DIM, N_REGION * LAT)
    query_grad = query_grad.reshape(N_REGION, HEADS, N_REGION, CAP, HEAD_DIM).astype(jnp.float32)
    projection_grad = jnp.einsum('dhsce,sdcf->hef', query_grad, observations.astype(jnp.float32))
    projection_grad = projection_grad.reshape(HEADS * HEAD_DIM, OBS_WIDTH) / N_REGION
    return (pair_grad, projection_grad)
```

```python
import functools
import math

import jax
import jax.numpy as jnp
from jax import lax
from jax.experimental import pallas as pl
from jax.experimental.pallas import tpu as pltpu
from jax.sharding import PartitionSpec as P

HEAD_DIM = 32
MESH = pl.DeviceIdType.MESH
F32 = jnp.float32
BF16 = jnp.bfloat16


def slot_of(source, here, chips):
    away = (source // 2 - here // 2 + chips) % chips
    half = away // (chips // 2)
    block = (away * (1 - half) + (chips - away) * half) % (chips // 2)
    return block * 4 + half * 2 + source % 2


def kernel(
    regions,
    columns,
    counts_ref,
    obs_hbm,
    cot_hbm,
    kv_ref,
    weight_ref,
    pair_ref,
    proj_ref,
    obs_buf,
    cot_buf,
    kv_next,
    key_rows,
    value_rows,
    key_cols,
    key_acc,
    value_acc,
    proj_acc,
    edge_out,
    edge_in,
    part_out,
    part_in,
    group_in,
    final_in,
    obs_recv,
    cot_recv,
    obs_send,
    relay_send,
    cot_send,
    own_sem,
    kv_sems,
    edge_sems,
    part_sems,
    group_sems,
    final_sems,
):
    chips = regions // 2
    me = lax.axis_index("region")
    col = lax.axis_index("mp")
    my_chip = me // 2
    my_core = me % 2
    latent = kv_ref.shape[2]
    shares = regions // columns
    blocks = regions // 4

    barrier = pltpu.get_barrier_semaphore()

    def greet_region(i, carry):
        peer = (me + i) % regions
        pl.semaphore_signal(barrier, inc=1, device_id=(peer, col), device_id_type=MESH)
        return carry

    def greet_column(i, carry):
        peer = (col + i) % columns
        pl.semaphore_signal(barrier, inc=1, device_id=(me, peer), device_id_type=MESH)
        return carry

    lax.fori_loop(1, regions, greet_region, 0)
    lax.fori_loop(1, columns, greet_column, 0)
    own_slot = my_core
    own_obs = pltpu.make_async_copy(obs_hbm.at[me], obs_buf.at[own_slot], obs_recv.at[own_slot])
    own_cot = pltpu.make_async_copy(cot_hbm.at[me], cot_buf.at[own_slot], cot_recv.at[own_slot])
    own_obs.start()
    own_cot.start()

    key_cols[...] = jnp.concatenate([kv_ref[0], kv_ref[0]], axis=1)
    pl.semaphore_wait(barrier, regions - 1 + columns - 1)

    kv_copy = pltpu.make_async_remote_copy(
        src_ref=kv_ref,
        dst_ref=kv_next,
        send_sem=kv_sems.at[0],
        recv_sem=kv_sems.at[1],
        device_id=((me + regions - 1) % regions, col),
        device_id_type=MESH,
    )
    kv_copy.start()

    first_share = (col - me + regions * columns) % columns

    def obs_copy(t):
        peer = first_share + columns * t
        slot = slot_of(me, peer, chips)
        return peer, pltpu.make_async_remote_copy(
            src_ref=obs_hbm.at[peer],
            dst_ref=obs_buf.at[slot],
            send_sem=obs_send.at[t],
            recv_sem=obs_recv.at[slot],
            device_id=(peer, col),
            device_id_type=MESH,
        )

    for t in range(shares):
        peer, copy = obs_copy(t)

        @pl.when(peer != me)
        def _():
            copy.start()

    def cot_copy(chip, core):
        peer = (chip % chips) * 2 + core
        slot = slot_of(me, peer, chips)
        return pltpu.make_async_remote_copy(
            src_ref=cot_hbm.at[peer],
            dst_ref=cot_buf.at[slot],
            send_sem=cot_send,
            recv_sem=cot_recv.at[slot],
            device_id=(peer, col),
            device_id_type=MESH,
        )

    cot_copy(my_chip, 1 - my_core).start()

    def send_at_distance(k, carry):
        for core in range(2):
            cot_copy(my_chip + k, core).start()
            cot_copy(my_chip + chips - k, core).start()
        return carry

    lax.fori_loop(1, chips // 2, send_at_distance, 0)
    for core in range(2):
        cot_copy(my_chip + chips // 2, core).start()

    def wait_obs(slot):
        pltpu.make_async_copy(obs_hbm.at[0], obs_buf.at[slot], obs_recv.at[slot]).wait()

    def wait_cot(slot):
        pltpu.make_async_copy(cot_hbm.at[0], cot_buf.at[slot], cot_recv.at[slot]).wait()

    for t in range(shares):
        source = first_share + columns * t
        slot = slot_of(source, me, chips)

        @pl.when(source != me)
        def _():
            wait_obs(slot)

            def relay(i, carry):
                pltpu.make_async_remote_copy(
                    src_ref=obs_buf.at[slot],
                    dst_ref=obs_buf.at[slot],
                    send_sem=relay_send.at[t],
                    recv_sem=obs_recv.at[slot],
                    device_id=(me, (col + i) % columns),
                    device_id_type=MESH,
                ).start()
                return carry

            lax.fori_loop(1, columns, relay, 0)

    kv_copy.wait_recv()
    key_cols[:, latent:] = kv_next[0]
    key_rows[...] = jnp.transpose(key_cols[...].astype(F32)).astype(BF16)
    values = jnp.concatenate([kv_ref[1], kv_next[1]], axis=1)
    values = jnp.transpose(values.astype(F32)).astype(BF16)
    value_rows[...] = jnp.concatenate([values] * 4, axis=1)
    key_acc[...] = jnp.zeros_like(key_acc)
    value_acc[...] = jnp.zeros_like(value_acc)
    proj_acc[...] = jnp.zeros_like(proj_acc)

    rows = 4 * obs_buf.shape[1]
    slots = obs_buf.shape[1]
    packed = cot_buf.shape[1]
    scale_back = 1.0 / math.sqrt(HEAD_DIM)
    power_scale = scale_back * math.log2(math.e)
    spread = (
        lax.broadcasted_iota(jnp.int32, (rows, 4 * packed), 0) // 4
        == lax.broadcasted_iota(jnp.int32, (rows, 4 * packed), 1)
    ).astype(F32).astype(BF16)

    def source_at(block, part):
        half = part // 2
        away = jnp.where(block == 0, half * (chips // 2), jnp.where(half == 0, block, chips - block))
        return ((my_chip + away) % chips) * 2 + part % 2

    def attend(step, carry):
        block = (step + 1) % blocks
        for part in range(4):
            slot = block * 4 + part
            source = source_at(block, part)

            if part < 2:
                wait_cot(slot)

                @pl.when(jnp.logical_or((source + me) % columns != col, source == me))
                def _():
                    wait_obs(slot)
            else:
                wait_cot(slot)

                @pl.when((source + me) % columns != col)
                def _():
                    wait_obs(slot)

        obs = obs_buf[pl.ds(block * 4, 4)].reshape(rows, obs_buf.shape[2])
        cot = cot_buf[pl.ds(block * 4, 4)].reshape(4 * packed, cot_buf.shape[2])
        query = lax.dot_general(
            obs, weight_ref[...], (((1,), (1,)), ((), ())), preferred_element_type=F32
        ).astype(BF16)
        grads = lax.dot_general(
            spread, cot, (((1,), (0,)), ((), ())), preferred_element_type=F32
        )
        row = lax.broadcasted_iota(jnp.int32, (slots, grads.shape[1]), 0)
        lane = lax.broadcasted_iota(jnp.int32, (slots, grads.shape[1]), 1)
        band = lane // HEAD_DIM == row % 4
        pieces = []
        for part in range(4):
            live = counts_ref[source_at(block, part), me]
            keep = jnp.logical_and(band, row < live)
            piece = grads[part * slots : (part + 1) * slots]
            pieces.append(jnp.where(keep, piece, 0.0))
        grads = jnp.concatenate(pieces, axis=0).astype(BF16)

        scores = lax.dot_general(
            key_rows[...], query, (((1,), (1,)), ((), ())), preferred_element_type=F32
        )
        top = jnp.max(scores, axis=0, keepdims=True)
        powers = jnp.exp2((scores - top) * power_scale)
        attention = powers * (1.0 / jnp.sum(powers, axis=0, keepdims=True))
        prob_grad = lax.dot_general(
            value_rows[...], grads, (((1,), (1,)), ((), ())), preferred_element_type=F32
        )
        row_dot = jnp.sum(attention * prob_grad, axis=0, keepdims=True)
        score_grad = (attention * (prob_grad - row_dot)).astype(BF16)
        key_acc[...] += jnp.dot(score_grad, query, preferred_element_type=F32)
        value_acc[...] += jnp.dot(attention.astype(BF16), grads, preferred_element_type=F32)
        query_grad = jnp.dot(key_cols[...], score_grad, preferred_element_type=F32)
        query_grad = (query_grad * scale_back).astype(BF16)
        proj_acc[...] += jnp.dot(query_grad, obs, preferred_element_type=F32)
        return carry

    lax.fori_loop(0, blocks, attend, 0)

    group = me // 8
    member = me % 8
    groups = regions // 8
    tiles = [(r, c) for r in range(0, proj_acc.shape[0], 8) for c in range(0, proj_acc.shape[1], 128)]
    for index, (r, c) in enumerate(tiles):
        part_out[index] = proj_acc[r : r + 8, c : c + 128]

    def part_copy(i):
        peer = (member + i) % 8
        return pltpu.make_async_remote_copy(
            src_ref=part_out.at[peer],
            dst_ref=part_in.at[i - 1],
            send_sem=part_sems.at[0, i - 1],
            recv_sem=part_sems.at[1, i - 1],
            device_id=(group * 8 + peer, col),
            device_id_type=MESH,
        )

    for i in range(1, 8):
        part_copy(i).start()

    key_grad = jnp.transpose(key_acc[...]) * scale_back
    value_grad = jnp.transpose(value_acc[...])
    value_grad = (value_grad[:HEAD_DIM] + value_grad[HEAD_DIM : 2 * HEAD_DIM]) + (
        value_grad[2 * HEAD_DIM : 3 * HEAD_DIM] + value_grad[3 * HEAD_DIM :]
    )
    edge_out[0] = key_grad[:, latent:].astype(BF16)
    edge_out[1] = value_grad[:, latent:].astype(BF16)
    edge_copy = pltpu.make_async_remote_copy(
        src_ref=edge_out,
        dst_ref=edge_in,
        send_sem=edge_sems.at[0],
        recv_sem=edge_sems.at[1],
        device_id=((me + 1) % regions, col),
        device_id_type=MESH,
    )
    edge_copy.start()
    pair_ref[0] = key_grad[:, :latent]
    pair_ref[1] = value_grad[:, :latent]

    for i in range(1, 8):
        part_copy(i).wait_recv()
    total = part_out[member]
    for i in range(1, 8):
        total = total + part_in[i - 1]
    group_in[group] = total

    def group_copy(i):
        peer = (group + i) % groups
        return pltpu.make_async_remote_copy(
            src_ref=group_in.at[group],
            dst_ref=group_in.at[group],
            send_sem=group_sems.at[0, i - 1],
            recv_sem=group_sems.at[1, group],
            device_id=(peer * 8 + member, col),
            device_id_type=MESH,
        )

    for i in range(1, groups):
        group_copy(i).start()

    edge_copy.wait_recv()
    pair_ref[...] += edge_in[...].astype(F32)

    for i in range(1, groups):
        peer = (group + i) % groups
        pltpu.make_async_copy(
            group_in.at[peer], group_in.at[peer], group_sems.at[1, peer]
        ).wait()
    total = group_in[0]
    for index in range(1, groups):
        total = total + group_in[index]
    final_in[member] = total * (1.0 / regions)

    def final_copy(i):
        peer = (member + i) % 8
        return pltpu.make_async_remote_copy(
            src_ref=final_in.at[member],
            dst_ref=final_in.at[member],
            send_sem=final_sems.at[0, i - 1],
            recv_sem=final_sems.at[1, member],
            device_id=(group * 8 + peer, col),
            device_id_type=MESH,
        )

    for i in range(1, 8):
        final_copy(i).start()
    for i in range(1, 8):
        peer = (member + i) % 8
        pltpu.make_async_copy(
            final_in.at[peer], final_in.at[peer], final_sems.at[1, peer]
        ).wait()
    for index, (r, c) in enumerate(tiles):
        proj_ref[r : r + 8, c : c + 128] = final_in[index]

    kv_copy.wait_send()
    edge_copy.wait_send()
    for t in range(shares):
        peer, copy = obs_copy(t)

        @pl.when(peer != me)
        def _():
            copy.wait_send()
            many = pl.ds(0, columns - 1)
            pltpu.make_async_copy(obs_buf.at[many], obs_buf.at[many], relay_send.at[t]).wait()

    many = pl.ds(0, regions - 1)
    pltpu.make_async_copy(cot_buf.at[many], cot_buf.at[many], cot_send).wait()
    for i in range(1, 8):
        part_copy(i).wait_send()
        final_copy(i).wait_send()
    for i in range(1, groups):
        group_copy(i).wait_send()


def per_device(observations, cotangent, keys_values, query_weight, counts):
    regions = lax.axis_size("region")
    columns = lax.axis_size("mp")
    capacity = observations.shape[2]
    width = observations.shape[3]
    latent = keys_values.shape[2]
    reach = 2 * latent
    packed = capacity * HEAD_DIM // 128
    cot = cotangent.reshape(regions, packed, 128)
    vmem = pl.BlockSpec(memory_space=pltpu.VMEM)
    hbm = pl.BlockSpec(memory_space=pl.ANY)
    dma = pltpu.SemaphoreType.DMA
    groups = regions // 8
    pair_grad, projection_grad = pl.pallas_call(
        functools.partial(kernel, regions, columns),
        name="region_backward",
        out_shape=(
            jax.ShapeDtypeStruct((2, HEAD_DIM, latent), F32),
            jax.ShapeDtypeStruct((HEAD_DIM, width), F32),
        ),
        in_specs=[pl.BlockSpec(memory_space=pltpu.SMEM), hbm, hbm, vmem, vmem],
        out_specs=(vmem, vmem),
        scratch_shapes=[
            pltpu.VMEM((regions, capacity, width), BF16),
            pltpu.VMEM((regions, packed, 128), BF16),
            pltpu.VMEM((2, HEAD_DIM, latent), BF16),
            pltpu.VMEM((reach, HEAD_DIM), BF16),
            pltpu.VMEM((reach, 4 * HEAD_DIM), BF16),
            pltpu.VMEM((HEAD_DIM, reach), BF16),
            pltpu.VMEM((reach, HEAD_DIM), F32),
            pltpu.VMEM((reach, 4 * HEAD_DIM), F32),
            pltpu.VMEM((HEAD_DIM, width), F32),
            pltpu.VMEM((2, HEAD_DIM, latent), BF16),
            pltpu.VMEM((2, HEAD_DIM, latent), BF16),
            pltpu.VMEM((8, 8, 128), F32),
            pltpu.VMEM((7, 8, 128), F32),
            pltpu.VMEM((groups, 8, 128), F32),
            pltpu.VMEM((8, 8, 128), F32),
            dma((regions,)),
            dma((regions,)),
            dma((regions // columns,)),
            dma((regions // columns,)),
            dma,
            dma((1,)),
            dma((2,)),
            dma((2,)),
            dma((2, 7)),
            dma((2, groups)),
            dma((2, 8)),
        ],
        compiler_params=pltpu.CompilerParams(collective_id=0, has_side_effects=True),
    )(counts, observations[0], cot, keys_values, query_weight)
    return (pair_grad, projection_grad)


def solution(mesh):
    in_specs = (
        P("region", None, None, None),
        P("region", None, "mp", None),
        P(None, "mp", "region"),
        P("mp", None),
        P(),
    )
    out_specs = (P(None, "mp", "region"), P("mp", None))
    return jax.shard_map(
        per_device, mesh=mesh, in_specs=in_specs, out_specs=out_specs, check_vma=False
    )
```

```python
import functools
import math

import jax
import jax.numpy as jnp
from jax import lax
from jax.experimental import pallas as pl
from jax.experimental.pallas import tpu as pltpu
from jax.sharding import PartitionSpec as P

HEAD_DIM = 32
FIRST_LAG = 3
SECOND_LAG = 6
MESH = pl.DeviceIdType.MESH
F32 = jnp.float32
BF16 = jnp.bfloat16


def slot_of(source, here, chips):
    away = (source // 2 - here // 2 + chips) % chips
    half = away // (chips // 2)
    block = (away * (1 - half) + (chips - away) * half) % (chips // 2)
    return block * 4 + half * 2 + source % 2


def kernel(
    regions,
    columns,
    counts_ref,
    obs_hbm,
    cot_hbm,
    kv_ref,
    weight_ref,
    pair_ref,
    proj_ref,
    obs_buf,
    cot_buf,
    kv_next,
    reach_rows,
    reach_cols,
    weight_rows,
    reach_acc,
    proj_acc,
    scores_buf,
    grads_buf,
    rows_buf,
    top_buf,
    edge_out,
    edge_in,
    part_out,
    part_in,
    group_in,
    final_in,
    obs_recv,
    cot_recv,
    obs_send,
    relay_send,
    cot_send,
    own_sem,
    kv_sems,
    edge_sems,
    part_sems,
    group_sems,
    final_sems,
):
    chips = regions // 2
    me = lax.axis_index("region")
    col = lax.axis_index("mp")
    my_chip = me // 2
    my_core = me % 2
    latent = kv_ref.shape[2]
    blocks = regions // 4

    across = 4
    def along_x(i):
        return (col // across) * across + (col % across + i) % across

    def along_y(i):
        return (col + i * across) % columns

    barrier = pltpu.get_barrier_semaphore()

    def tell(sem, region, column):
        pl.semaphore_signal(sem, inc=1, device_id=(region, column), device_id_type=MESH)

    def greet_region(i, carry):
        tell(barrier, (me + i) % regions, col)
        return carry

    lax.fori_loop(1, regions, greet_region, 0)
    for i in range(1, across):
        tell(barrier, me, along_x(i))
        tell(barrier, me, along_y(i))
    own_slot = my_core
    own_obs = pltpu.make_async_copy(obs_hbm.at[me], obs_buf.at[own_slot], obs_recv.at[own_slot])
    own_cot = pltpu.make_async_copy(cot_hbm.at[me], cot_buf.at[own_slot], cot_recv.at[own_slot])
    own_obs.start()
    own_cot.start()

    reach_cols[:HEAD_DIM, :latent] = kv_ref[0]
    reach_cols[HEAD_DIM:, :latent] = kv_ref[1]
    weight_rows[:HEAD_DIM] = weight_ref[...]
    weight_rows[HEAD_DIM:] = jnp.zeros_like(weight_ref)
    reach_acc[...] = jnp.zeros_like(reach_acc)
    proj_acc[...] = jnp.zeros_like(proj_acc)
    for ref in (*scores_buf, *grads_buf, *rows_buf, *top_buf):
        ref[...] = jnp.zeros_like(ref)
    pl.semaphore_wait(barrier, regions - 1 + 2 * (across - 1))
    kv_copy = pltpu.make_async_remote_copy(
        src_ref=kv_ref,
        dst_ref=kv_next,
        send_sem=kv_sems.at[0],
        recv_sem=kv_sems.at[1],
        device_id=((me + regions - 1) % regions, col),
        device_id_type=MESH,
    )

    def obs_copy(peer):
        slot = slot_of(me, peer, chips)
        return pltpu.make_async_remote_copy(
            src_ref=obs_hbm.at[peer],
            dst_ref=obs_buf.at[slot],
            send_sem=obs_send.at[peer // columns],
            recv_sem=obs_recv.at[slot],
            device_id=(peer, col),
            device_id_type=MESH,
        )

    def cot_copy(chip, core):
        peer = (chip % chips) * 2 + core
        slot = slot_of(me, peer, chips)
        return pltpu.make_async_remote_copy(
            src_ref=cot_hbm.at[peer],
            dst_ref=cot_buf.at[slot],
            send_sem=cot_send,
            recv_sem=cot_recv.at[slot],
            device_id=(peer, col),
            device_id_type=MESH,
        )

    kv_copy.start()
    for t in range(regions // columns):
        peer = (col - me + regions * columns) % columns + columns * t

        @pl.when(peer != me)
        def _():
            obs_copy(peer).start()

    def send_at_distance(k, carry):
        for core in range(2):
            cot_copy(my_chip + k, core).start()
            cot_copy(my_chip + chips - k, core).start()
        return carry

    cot_copy(my_chip, 1 - my_core).start()
    lax.fori_loop(1, chips // 2, send_at_distance, 0)
    for core in range(2):
        cot_copy(my_chip + chips // 2, core).start()

    def wait_obs(slot):
        pltpu.make_async_copy(obs_hbm.at[0], obs_buf.at[slot], obs_recv.at[slot]).wait()

    def wait_cot(slot):
        pltpu.make_async_copy(cot_hbm.at[0], cot_buf.at[slot], cot_recv.at[slot]).wait()

    kv_copy.wait_recv()
    reach_cols[:HEAD_DIM, latent:] = kv_next[0]
    reach_cols[HEAD_DIM:, latent:] = kv_next[1]
    reach_rows[...] = jnp.transpose(reach_cols[...].astype(F32)).astype(BF16)

    rows = 4 * obs_buf.shape[1]
    slots = obs_buf.shape[1]
    packed = cot_buf.shape[1]
    scale_back = 1.0 / math.sqrt(HEAD_DIM)
    power_scale = scale_back * math.log2(math.e)
    spread = (
        lax.broadcasted_iota(jnp.int32, (rows, 4 * packed), 0) // 4
        == lax.broadcasted_iota(jnp.int32, (rows, 4 * packed), 1)
    ).astype(F32).astype(BF16)

    fold = (
        lax.broadcasted_iota(jnp.int32, (4 * HEAD_DIM, 2 * HEAD_DIM), 0) % HEAD_DIM + HEAD_DIM
        == lax.broadcasted_iota(jnp.int32, (4 * HEAD_DIM, 2 * HEAD_DIM), 1)
    ).astype(F32).astype(BF16)
    row = lax.broadcasted_iota(jnp.int32, (slots, 4 * HEAD_DIM), 0)
    lane = lax.broadcasted_iota(jnp.int32, (slots, 4 * HEAD_DIM), 1)
    band = lane // HEAD_DIM == row % 4
    chunk = 128
    chunks = 2 * latent // chunk

    def source_at(block, part):
        half = part // 2
        away = jnp.where(block == 0, half * (chips // 2), jnp.where(half == 0, block, chips - block))
        return ((my_chip + away) % chips) * 2 + part % 2

    def relay(slot, peer):
        pltpu.make_async_remote_copy(
            src_ref=obs_buf.at[slot],
            dst_ref=obs_buf.at[slot],
            send_sem=relay_send.at[slot],
            recv_sem=obs_recv.at[slot],
            device_id=(me, peer),
            device_id_type=MESH,
        ).start()

    def in_line(part, owner):
        if part < 2:
            return owner // across == col // across
        return owner % across == col % across

    def each_part(block):
        for part in range(4):
            source = source_at(block, part)
            yield part, block * 4 + part, source, (source + me) % columns

    def spread_first(block):
        for part, slot, source, owner in each_part(block):

            @pl.when(jnp.logical_and(owner == col, source != me))
            def _():
                wait_obs(slot)
                for i in range(1, across):
                    relay(slot, along_x(i) if part < 2 else along_y(i))

    def spread_second(block):
        for part, slot, source, owner in each_part(block):

            @pl.when(jnp.logical_and(in_line(part, owner), source != me))
            def _():
                @pl.when(owner != col)
                def _():
                    wait_obs(slot)

                for i in range(1, across):
                    relay(slot, along_y(i) if part < 2 else along_x(i))

    def arrived(block):
        for part, slot, source, owner in each_part(block):
            wait_cot(slot)

            @pl.when(jnp.logical_or(jnp.logical_not(in_line(part, owner)), source == me))
            def _():
                wait_obs(slot)

    def block_obs(block):
        return obs_buf[pl.ds(block * 4, 4)].reshape(rows, obs_buf.shape[2])

    def fold_rows(value):
        return value.reshape(chunk // 8, 8, rows)

    def compute(block, last, even):
        scores_now, scores_before = scores_buf[even], scores_buf[1 - even]
        grads_now, grads_before = grads_buf[1 - even], grads_buf[even]
        rows_ref = rows_buf[even]
        top = jnp.max(top_buf[1 - even][...], axis=0, keepdims=True)
        total = jnp.zeros((8, rows), F32)
        row_dot = jnp.zeros((8, rows), F32)
        query_grad = jnp.zeros((HEAD_DIM, rows), F32)
        for index in range(chunks):
            where = slice(index * chunk, (index + 1) * chunk)
            powers = jnp.exp2((scores_before[where, :rows] - top) * power_scale)
            scores_before[where, :rows] = powers
            total = total + jnp.sum(fold_rows(powers), axis=0)
            row_dot = row_dot + jnp.sum(fold_rows(powers * scores_before[where, rows:]), axis=0)
            reach_acc[where] += jnp.dot(
                grads_before[where], rows_ref[...], preferred_element_type=F32
            )
            if index % 2:
                pair = slice((index - 1) * chunk, (index + 1) * chunk)
                query_grad = query_grad + jnp.dot(
                    reach_cols[:HEAD_DIM, pair],
                    grads_before[pair, :rows],
                    preferred_element_type=F32,
                )
            if index == 1:
                cot = cot_buf[pl.ds(block * 4, 4)].reshape(4 * packed, cot_buf.shape[2])
                query = lax.dot_general(
                    block_obs(block),
                    weight_rows[...],
                    (((1,), (1,)), ((), ())),
                    preferred_element_type=F32,
                ).astype(BF16)
                wide = jnp.dot(spread, cot, preferred_element_type=F32)
                pieces = []
                for part in range(4):
                    live = counts_ref[source_at(block, part), me]
                    keep = jnp.logical_and(band, row < live)
                    pieces.append(jnp.where(keep, wide[part * slots : (part + 1) * slots], 0.0))
                wide = jnp.concatenate(pieces, axis=0).astype(BF16)
            if index == 4:
                grads = jnp.dot(wide, fold, preferred_element_type=F32).astype(BF16)
        rows_ref[:rows] = query
        rows_ref[rows:] = grads
        both = jnp.concatenate([query, grads], axis=0)
        inverse = 1.0 / jnp.sum(total, axis=0, keepdims=True)
        row_dot = jnp.sum(row_dot, axis=0, keepdims=True) * inverse
        query_grad = (query_grad * scale_back).astype(BF16)
        highest = None
        for index in range(chunks):
            where = slice(index * chunk, (index + 1) * chunk)
            products = lax.dot_general(
                reach_rows[where], both, (((1,), (1,)), ((), ())), preferred_element_type=F32
            )
            scores_now[where] = products
            here = jnp.max(fold_rows(products[:, :rows]), axis=0)
            highest = here if highest is None else jnp.maximum(highest, here)
            attention = scores_before[where, :rows] * inverse
            score_grad = attention * (scores_before[where, rows:] - row_dot)
            grads_now[where, :rows] = score_grad.astype(BF16)
            grads_now[where, rows:] = attention.astype(BF16)
            if index == 3:
                proj_acc[...] += jnp.dot(query_grad, block_obs(last), preferred_element_type=F32)
        top_buf[even][...] = highest

    def at(index):
        return (jnp.clip(index, 0, blocks - 1) + 1) % blocks

    def stage(step, even):
        @pl.when(step < blocks)
        def _():
            spread_first((step + 1) % blocks)

        @pl.when(jnp.logical_and(step >= FIRST_LAG, step < blocks + FIRST_LAG))
        def _():
            spread_second((step - FIRST_LAG + 1) % blocks)

        index = step - SECOND_LAG

        @pl.when(jnp.logical_and(index >= 0, index < blocks))
        def _():
            arrived(at(index))

        @pl.when(index >= 0)
        def _():
            compute(at(index), at(index - 2), even)

    def stages(pair, carry):
        for even in range(2):
            stage(pair * 2 + even, even)
        return carry

    lax.fori_loop(0, (blocks + 2 + SECOND_LAG) // 2, stages, 0)

    group = me // 8
    member = me % 8
    groups = regions // 8
    tiles = [(r, c) for r in range(0, proj_acc.shape[0], 8) for c in range(0, proj_acc.shape[1], 128)]
    for index, (r, c) in enumerate(tiles):
        part_out[index] = proj_acc[r : r + 8, c : c + 128]

    def part_copy(i):
        peer = (member + i) % 8
        return pltpu.make_async_remote_copy(
            src_ref=part_out.at[peer],
            dst_ref=part_in.at[i - 1],
            send_sem=part_sems.at[0, i - 1],
            recv_sem=part_sems.at[1, i - 1],
            device_id=(group * 8 + peer, col),
            device_id_type=MESH,
        )

    for i in range(1, 8):
        part_copy(i).start()

    reach_grad = jnp.transpose(reach_acc[...])
    key_grad = reach_grad[:HEAD_DIM] * scale_back
    value_grad = reach_grad[HEAD_DIM:]
    edge_out[0] = key_grad[:, latent:].astype(BF16)
    edge_out[1] = value_grad[:, latent:].astype(BF16)
    edge_copy = pltpu.make_async_remote_copy(
        src_ref=edge_out,
        dst_ref=edge_in,
        send_sem=edge_sems.at[0],
        recv_sem=edge_sems.at[1],
        device_id=((me + 1) % regions, col),
        device_id_type=MESH,
    )
    edge_copy.start()
    pair_ref[0] = key_grad[:, :latent]
    pair_ref[1] = value_grad[:, :latent]

    for i in range(1, 8):
        part_copy(i).wait_recv()
    total = part_out[member]
    for i in range(1, 8):
        total = total + part_in[i - 1]
    group_in[group] = total

    def group_copy(i):
        peer = (group + i) % groups
        return pltpu.make_async_remote_copy(
            src_ref=group_in.at[group],
            dst_ref=group_in.at[group],
            send_sem=group_sems.at[0, i - 1],
            recv_sem=group_sems.at[1, group],
            device_id=(peer * 8 + member, col),
            device_id_type=MESH,
        )

    for i in range(1, groups):
        group_copy(i).start()

    def sent_block(block, carry):
        for part, slot, source, owner in each_part(block):

            @pl.when(jnp.logical_and(owner == col, source != me))
            def _():
                obs_copy(source).wait_send()
                many = pl.ds(0, 2 * across - 2)
                pltpu.make_async_copy(obs_buf.at[many], obs_buf.at[many], relay_send.at[slot]).wait()

            @pl.when(
                jnp.logical_and(
                    jnp.logical_and(in_line(part, owner), owner != col), source != me
                )
            )
            def _():
                many = pl.ds(0, across - 1)
                pltpu.make_async_copy(obs_buf.at[many], obs_buf.at[many], relay_send.at[slot]).wait()

        return carry

    lax.fori_loop(0, blocks, sent_block, 0)
    edge_copy.wait_recv()
    pair_ref[...] += edge_in[...].astype(F32)

    for i in range(1, groups):
        peer = (group + i) % groups
        pltpu.make_async_copy(
            group_in.at[peer], group_in.at[peer], group_sems.at[1, peer]
        ).wait()
    total = group_in[0]
    for index in range(1, groups):
        total = total + group_in[index]
    final_in[member] = total * (1.0 / regions)

    def final_copy(i):
        peer = (member + i) % 8
        return pltpu.make_async_remote_copy(
            src_ref=final_in.at[member],
            dst_ref=final_in.at[member],
            send_sem=final_sems.at[0, i - 1],
            recv_sem=final_sems.at[1, member],
            device_id=(group * 8 + peer, col),
            device_id_type=MESH,
        )

    for i in range(1, 8):
        final_copy(i).start()
    for i in range(1, 8):
        peer = (member + i) % 8
        pltpu.make_async_copy(
            final_in.at[peer], final_in.at[peer], final_sems.at[1, peer]
        ).wait()
    for index, (r, c) in enumerate(tiles):
        proj_ref[r : r + 8, c : c + 128] = final_in[index]

    kv_copy.wait_send()
    edge_copy.wait_send()
    many = pl.ds(0, regions - 1)
    pltpu.make_async_copy(cot_buf.at[many], cot_buf.at[many], cot_send).wait()
    for i in range(1, 8):
        part_copy(i).wait_send()
        final_copy(i).wait_send()
    for i in range(1, groups):
        group_copy(i).wait_send()


def per_device(observations, cotangent, keys_values, query_weight, counts):
    regions = lax.axis_size("region")
    columns = lax.axis_size("mp")
    capacity = observations.shape[2]
    width = observations.shape[3]
    latent = keys_values.shape[2]
    reach = 2 * latent
    packed = capacity * HEAD_DIM // 128
    cot = cotangent.reshape(regions, packed, 128)
    vmem = pl.BlockSpec(memory_space=pltpu.VMEM)
    hbm = pl.BlockSpec(memory_space=pl.ANY)
    dma = pltpu.SemaphoreType.DMA
    groups = regions // 8
    pair_grad, projection_grad = pl.pallas_call(
        functools.partial(kernel, regions, columns),
        name="region_backward",
        out_shape=(
            jax.ShapeDtypeStruct((2, HEAD_DIM, latent), F32),
            jax.ShapeDtypeStruct((HEAD_DIM, width), F32),
        ),
        in_specs=[pl.BlockSpec(memory_space=pltpu.SMEM), hbm, hbm, vmem, vmem],
        out_specs=(vmem, vmem),
        scratch_shapes=[
            pltpu.VMEM((regions, capacity, width), BF16),
            pltpu.VMEM((regions, packed, 128), BF16),
            pltpu.VMEM((2, HEAD_DIM, latent), BF16),
            pltpu.VMEM((reach, 2 * HEAD_DIM), BF16),
            pltpu.VMEM((2 * HEAD_DIM, reach), BF16),
            pltpu.VMEM((2 * HEAD_DIM, width), BF16),
            pltpu.VMEM((reach, 2 * HEAD_DIM), F32),
            pltpu.VMEM((HEAD_DIM, width), F32),
            [pltpu.VMEM((reach, 8 * capacity), F32)] * 2,
            [pltpu.VMEM((reach, 8 * capacity), BF16)] * 2,
            [pltpu.VMEM((8 * capacity, 2 * HEAD_DIM), BF16)] * 2,
            [pltpu.VMEM((8, 4 * capacity), F32)] * 2,
            pltpu.VMEM((2, HEAD_DIM, latent), BF16),
            pltpu.VMEM((2, HEAD_DIM, latent), BF16),
            pltpu.VMEM((8, 8, 128), F32),
            pltpu.VMEM((7, 8, 128), F32),
            pltpu.VMEM((groups, 8, 128), F32),
            pltpu.VMEM((8, 8, 128), F32),
            dma((regions,)),
            dma((regions,)),
            dma((regions // columns,)),
            dma((regions,)),
            dma,
            dma((1,)),
            dma((2,)),
            dma((2,)),
            dma((2, 7)),
            dma((2, groups)),
            dma((2, 8)),
        ],
        compiler_params=pltpu.CompilerParams(collective_id=0, has_side_effects=True),
    )(counts, observations[0], cot, keys_values, query_weight)
    return (pair_grad, projection_grad)


def solution(mesh):
    in_specs = (
        P("region", None, None, None),
        P("region", None, "mp", None),
        P(None, "mp", "region"),
        P("mp", None),
        P(),
    )
    out_specs = (P(None, "mp", "region"), P("mp", None))
    return jax.shard_map(
        per_device, mesh=mesh, in_specs=in_specs, out_specs=out_specs, check_vma=False
    )
```

```python
import functools
import math

import jax
import jax.numpy as jnp
from jax import lax
from jax.experimental import pallas as pl
from jax.experimental.pallas import tpu as pltpu
from jax.sharding import PartitionSpec as P

HEAD_DIM = 32
FIRST_LAG = 3
SECOND_LAG = 6
MESH = pl.DeviceIdType.MESH
F32 = jnp.float32
BF16 = jnp.bfloat16


def slot_of(source, here, chips):
    away = (source // 2 - here // 2 + chips) % chips
    half = away // (chips // 2)
    block = (away * (1 - half) + (chips - away) * half) % (chips // 2)
    return block * 4 + half * 2 + source % 2


def kernel(
    regions,
    columns,
    counts_ref,
    obs_hbm,
    cot_hbm,
    kv_ref,
    weight_ref,
    pair_ref,
    proj_ref,
    obs_buf,
    cot_buf,
    kv_next,
    reach_rows,
    reach_cols,
    weight_rows,
    reach_acc,
    proj_acc,
    scores_buf,
    grads_buf,
    rows_buf,
    top_buf,
    edge_out,
    edge_in,
    part_out,
    part_in,
    group_in,
    final_in,
    obs_recv,
    cot_recv,
    obs_send,
    relay_send,
    cot_send,
    own_sem,
    kv_sems,
    edge_sems,
    part_sems,
    group_sems,
    final_sems,
):
    chips = regions // 2
    me = lax.axis_index("region")
    col = lax.axis_index("mp")
    my_chip = me // 2
    my_core = me % 2
    latent = kv_ref.shape[2]
    blocks = regions // 4

    across = 4
    def along_x(i):
        return (col // across) * across + (col % across + i) % across

    def along_y(i):
        return (col + i * across) % columns

    barrier = pltpu.get_barrier_semaphore()

    def tell(sem, region, column):
        pl.semaphore_signal(sem, inc=1, device_id=(region, column), device_id_type=MESH)

    def greet_region(i, carry):
        tell(barrier, (me + i) % regions, col)
        return carry

    lax.fori_loop(1, regions, greet_region, 0)
    for i in range(1, across):
        tell(barrier, me, along_x(i))
        tell(barrier, me, along_y(i))
    own_slot = my_core
    own_obs = pltpu.make_async_copy(obs_hbm.at[me], obs_buf.at[own_slot], obs_recv.at[own_slot])
    own_cot = pltpu.make_async_copy(cot_hbm.at[me], cot_buf.at[own_slot], cot_recv.at[own_slot])
    own_obs.start()
    own_cot.start()

    pl.semaphore_wait(barrier, regions - 1 + 2 * (across - 1))
    kv_copy = pltpu.make_async_remote_copy(
        src_ref=kv_ref,
        dst_ref=kv_next,
        send_sem=kv_sems.at[0],
        recv_sem=kv_sems.at[1],
        device_id=((me + regions - 1) % regions, col),
        device_id_type=MESH,
    )

    def obs_copy(peer):
        slot = slot_of(me, peer, chips)
        return pltpu.make_async_remote_copy(
            src_ref=obs_hbm.at[peer],
            dst_ref=obs_buf.at[slot],
            send_sem=obs_send.at[peer // columns],
            recv_sem=obs_recv.at[slot],
            device_id=(peer, col),
            device_id_type=MESH,
        )

    def cot_copy(chip, core):
        peer = (chip % chips) * 2 + core
        slot = slot_of(me, peer, chips)
        return pltpu.make_async_remote_copy(
            src_ref=cot_hbm.at[peer],
            dst_ref=cot_buf.at[slot],
            send_sem=cot_send,
            recv_sem=cot_recv.at[slot],
            device_id=(peer, col),
            device_id_type=MESH,
        )

    kv_copy.start()
    def send_obs(share):
        peer = (me + (col - 2 * me + 2 * regions) % columns + columns * share) % regions

        @pl.when(peer != me)
        def _():
            obs_copy(peer).start()

    def send_at_distance(k, carry):
        for core in range(2):
            cot_copy(my_chip + k, core).start()
            cot_copy(my_chip + chips - k, core).start()
        return carry

    send_obs(0)
    send_obs(3)
    send_obs(1)
    send_obs(2)
    cot_copy(my_chip, 1 - my_core).start()
    lax.fori_loop(1, chips // 2, send_at_distance, 0)
    for core in range(2):
        cot_copy(my_chip + chips // 2, core).start()

    def wait_obs(slot):
        pltpu.make_async_copy(obs_hbm.at[0], obs_buf.at[slot], obs_recv.at[slot]).wait()

    def wait_cot(slot):
        pltpu.make_async_copy(cot_hbm.at[0], cot_buf.at[slot], cot_recv.at[slot]).wait()

    reach_cols[:HEAD_DIM, :latent] = kv_ref[0]
    reach_cols[HEAD_DIM:, :latent] = kv_ref[1]
    weight_rows[:HEAD_DIM] = weight_ref[...]
    weight_rows[HEAD_DIM:] = jnp.zeros_like(weight_ref)
    reach_acc[...] = jnp.zeros_like(reach_acc)
    proj_acc[...] = jnp.zeros_like(proj_acc)
    for ref in (*scores_buf, *grads_buf, *rows_buf, *top_buf):
        ref[...] = jnp.zeros_like(ref)
    kv_copy.wait_recv()
    reach_cols[:HEAD_DIM, latent:] = kv_next[0]
    reach_cols[HEAD_DIM:, latent:] = kv_next[1]
    reach_rows[...] = jnp.transpose(reach_cols[...].astype(F32)).astype(BF16)

    rows = 4 * obs_buf.shape[1]
    slots = obs_buf.shape[1]
    packed = cot_buf.shape[1]
    scale_back = 1.0 / math.sqrt(HEAD_DIM)
    power_scale = scale_back * math.log2(math.e)
    spread = (
        lax.broadcasted_iota(jnp.int32, (rows, 4 * packed), 0) // 4
        == lax.broadcasted_iota(jnp.int32, (rows, 4 * packed), 1)
    ).astype(F32).astype(BF16)

    fold = (
        lax.broadcasted_iota(jnp.int32, (4 * HEAD_DIM, 2 * HEAD_DIM), 0) % HEAD_DIM + HEAD_DIM
        == lax.broadcasted_iota(jnp.int32, (4 * HEAD_DIM, 2 * HEAD_DIM), 1)
    ).astype(F32).astype(BF16)
    row = lax.broadcasted_iota(jnp.int32, (slots, 4 * HEAD_DIM), 0)
    lane = lax.broadcasted_iota(jnp.int32, (slots, 4 * HEAD_DIM), 1)
    band = lane // HEAD_DIM == row % 4
    chunk = 128
    chunks = 2 * latent // chunk

    def source_at(block, part):
        half = part // 2
        away = jnp.where(block == 0, half * (chips // 2), jnp.where(half == 0, block, chips - block))
        return ((my_chip + away) % chips) * 2 + part % 2

    def relay(slot, peer):
        pltpu.make_async_remote_copy(
            src_ref=obs_buf.at[slot],
            dst_ref=obs_buf.at[slot],
            send_sem=relay_send.at[slot],
            recv_sem=obs_recv.at[slot],
            device_id=(me, peer),
            device_id_type=MESH,
        ).start()

    def in_line(part, owner):
        if part < 2:
            return owner // across == col // across
        return owner % across == col % across

    def each_part(block):
        for part in range(4):
            source = source_at(block, part)
            yield part, block * 4 + part, source, (source + me) % columns

    def spread_first(block):
        for part, slot, source, owner in each_part(block):

            @pl.when(jnp.logical_and(owner == col, source != me))
            def _():
                wait_obs(slot)
                for i in range(1, across):
                    relay(slot, along_x(i) if part < 2 else along_y(i))

    def spread_second(block):
        for part, slot, source, owner in each_part(block):

            @pl.when(jnp.logical_and(in_line(part, owner), source != me))
            def _():
                @pl.when(owner != col)
                def _():
                    wait_obs(slot)

                for i in range(1, across):
                    relay(slot, along_y(i) if part < 2 else along_x(i))

    def arrived(block):
        for part, slot, source, owner in each_part(block):
            wait_cot(slot)

            @pl.when(jnp.logical_or(jnp.logical_not(in_line(part, owner)), source == me))
            def _():
                wait_obs(slot)

    def block_obs(block):
        return obs_buf[pl.ds(block * 4, 4)].reshape(rows, obs_buf.shape[2])

    def fold_rows(value):
        return value.reshape(chunk // 8, 8, rows)

    def compute(block, last, even, front=True, middle=True):
        scores_now, scores_before = scores_buf[even], scores_buf[1 - even]
        grads_now, grads_before = grads_buf[1 - even], grads_buf[even]
        rows_ref = rows_buf[even]
        top = jnp.max(top_buf[1 - even][...], axis=0, keepdims=True)
        total = jnp.zeros((8, rows), F32)
        row_dot = jnp.zeros((8, rows), F32)
        query_grad = jnp.zeros((HEAD_DIM, rows), F32)
        for index in range(chunks):
            where = slice(index * chunk, (index + 1) * chunk)
            if middle:
                powers = jnp.exp2((scores_before[where, :rows] - top) * power_scale)
                scores_before[where, :rows] = powers
                total = total + jnp.sum(fold_rows(powers), axis=0)
                row_dot = row_dot + jnp.sum(fold_rows(powers * scores_before[where, rows:]), axis=0)
            reach_acc[where] += jnp.dot(
                grads_before[where], rows_ref[...], preferred_element_type=F32
            )
            if index % 2:
                pair = slice((index - 1) * chunk, (index + 1) * chunk)
                query_grad = query_grad + jnp.dot(
                    reach_cols[:HEAD_DIM, pair],
                    grads_before[pair, :rows],
                    preferred_element_type=F32,
                )
            if front and index == 1:
                cot = cot_buf[pl.ds(block * 4, 4)].reshape(4 * packed, cot_buf.shape[2])
                query = lax.dot_general(
                    block_obs(block),
                    weight_rows[...],
                    (((1,), (1,)), ((), ())),
                    preferred_element_type=F32,
                ).astype(BF16)
                wide = jnp.dot(spread, cot, preferred_element_type=F32)
                pieces = []
                for part in range(4):
                    live = counts_ref[source_at(block, part), me]
                    keep = jnp.logical_and(band, row < live)
                    pieces.append(jnp.where(keep, wide[part * slots : (part + 1) * slots], 0.0))
                wide = jnp.concatenate(pieces, axis=0).astype(BF16)
            if front and index == 4:
                grads = jnp.dot(wide, fold, preferred_element_type=F32).astype(BF16)
        if front:
            rows_ref[:rows] = query
            rows_ref[rows:] = grads
            both = jnp.concatenate([query, grads], axis=0)
        if middle:
            inverse = 1.0 / jnp.sum(total, axis=0, keepdims=True)
            row_dot = jnp.sum(row_dot, axis=0, keepdims=True) * inverse
        query_grad = (query_grad * scale_back).astype(BF16)
        highest = None
        for index in range(chunks):
            where = slice(index * chunk, (index + 1) * chunk)
            if front:
                products = lax.dot_general(
                    reach_rows[where], both, (((1,), (1,)), ((), ())), preferred_element_type=F32
                )
                scores_now[where] = products
                here = jnp.max(fold_rows(products[:, :rows]), axis=0)
                highest = here if highest is None else jnp.maximum(highest, here)
            if middle:
                attention = scores_before[where, :rows] * inverse
                score_grad = attention * (scores_before[where, rows:] - row_dot)
                grads_now[where, :rows] = score_grad.astype(BF16)
                grads_now[where, rows:] = attention.astype(BF16)
            if index == 3:
                proj_acc[...] += jnp.dot(query_grad, block_obs(last), preferred_element_type=F32)
        if front:
            top_buf[even][...] = highest

    def at(index):
        return (jnp.clip(index, 0, blocks - 1) + 1) % blocks

    def stage(step, even):
        @pl.when(step < blocks)
        def _():
            spread_first((step + 1) % blocks)

        @pl.when(jnp.logical_and(step >= FIRST_LAG, step < blocks + FIRST_LAG))
        def _():
            spread_second((step - FIRST_LAG + 1) % blocks)

        index = step - SECOND_LAG

        @pl.when(jnp.logical_and(index >= 0, index < blocks))
        def _():
            arrived(at(index))

        @pl.when(index >= 0)
        def _():
            compute(at(index), at(index - 2), even)

    def stages(pair, carry):
        for even in range(2):
            stage(pair * 2 + even, even)
        return carry

    lax.fori_loop(0, (blocks + SECOND_LAG) // 2, stages, 0)
    compute(0, at(blocks - 2), 0, front=False)
    compute(0, at(blocks - 1), 1, front=False, middle=False)

    group = me // 8
    member = me % 8
    groups = regions // 8
    tiles = [(r, c) for r in range(0, proj_acc.shape[0], 8) for c in range(0, proj_acc.shape[1], 128)]
    for index, (r, c) in enumerate(tiles):
        part_out[index] = proj_acc[r : r + 8, c : c + 128]

    def part_copy(i):
        peer = (member + i) % 8
        return pltpu.make_async_remote_copy(
            src_ref=part_out.at[peer],
            dst_ref=part_in.at[i - 1],
            send_sem=part_sems.at[0, i - 1],
            recv_sem=part_sems.at[1, i - 1],
            device_id=(group * 8 + peer, col),
            device_id_type=MESH,
        )

    for i in range(1, 8):
        part_copy(i).start()

    reach_grad = jnp.transpose(reach_acc[...])
    key_grad = reach_grad[:HEAD_DIM] * scale_back
    value_grad = reach_grad[HEAD_DIM:]
    edge_out[0] = key_grad[:, latent:].astype(BF16)
    edge_out[1] = value_grad[:, latent:].astype(BF16)
    edge_copy = pltpu.make_async_remote_copy(
        src_ref=edge_out,
        dst_ref=edge_in,
        send_sem=edge_sems.at[0],
        recv_sem=edge_sems.at[1],
        device_id=((me + 1) % regions, col),
        device_id_type=MESH,
    )
    edge_copy.start()
    pair_ref[0] = key_grad[:, :latent]
    pair_ref[1] = value_grad[:, :latent]

    for i in range(1, 8):
        part_copy(i).wait_recv()
    total = part_out[member]
    for i in range(1, 8):
        total = total + part_in[i - 1]
    group_in[group] = total

    def group_copy(i):
        peer = (group + i) % groups
        return pltpu.make_async_remote_copy(
            src_ref=group_in.at[group],
            dst_ref=group_in.at[group],
            send_sem=group_sems.at[0, i - 1],
            recv_sem=group_sems.at[1, group],
            device_id=(peer * 8 + member, col),
            device_id_type=MESH,
        )

    for i in range(1, groups):
        group_copy(i).start()

    def sent_block(block, carry):
        for part, slot, source, owner in each_part(block):

            @pl.when(jnp.logical_and(owner == col, source != me))
            def _():
                obs_copy(source).wait_send()
                many = pl.ds(0, 2 * across - 2)
                pltpu.make_async_copy(obs_buf.at[many], obs_buf.at[many], relay_send.at[slot]).wait()

            @pl.when(
                jnp.logical_and(
                    jnp.logical_and(in_line(part, owner), owner != col), source != me
                )
            )
            def _():
                many = pl.ds(0, across - 1)
                pltpu.make_async_copy(obs_buf.at[many], obs_buf.at[many], relay_send.at[slot]).wait()

        return carry

    lax.fori_loop(0, blocks, sent_block, 0)
    edge_copy.wait_recv()
    pair_ref[...] += edge_in[...].astype(F32)

    for i in range(1, groups):
        peer = (group + i) % groups
        pltpu.make_async_copy(
            group_in.at[peer], group_in.at[peer], group_sems.at[1, peer]
        ).wait()
    total = group_in[0]
    for index in range(1, groups):
        total = total + group_in[index]
    final_in[member] = total * (1.0 / regions)

    def final_copy(i):
        peer = (member + i) % 8
        return pltpu.make_async_remote_copy(
            src_ref=final_in.at[member],
            dst_ref=final_in.at[member],
            send_sem=final_sems.at[0, i - 1],
            recv_sem=final_sems.at[1, member],
            device_id=(group * 8 + peer, col),
            device_id_type=MESH,
        )

    for i in range(1, 8):
        final_copy(i).start()
    for i in range(1, 8):
        peer = (member + i) % 8
        pltpu.make_async_copy(
            final_in.at[peer], final_in.at[peer], final_sems.at[1, peer]
        ).wait()
    for index, (r, c) in enumerate(tiles):
        proj_ref[r : r + 8, c : c + 128] = final_in[index]

    kv_copy.wait_send()
    edge_copy.wait_send()
    many = pl.ds(0, regions - 1)
    pltpu.make_async_copy(cot_buf.at[many], cot_buf.at[many], cot_send).wait()
    for i in range(1, 8):
        part_copy(i).wait_send()
        final_copy(i).wait_send()
    for i in range(1, groups):
        group_copy(i).wait_send()


def hand_over(pair_in, proj_in, pair_out, proj_out):
    pair_out[...] = pair_in[...]
    proj_out[...] = proj_in[...]


def per_device(observations, cotangent, keys_values, query_weight, counts):
    regions = lax.axis_size("region")
    columns = lax.axis_size("mp")
    capacity = observations.shape[2]
    width = observations.shape[3]
    latent = keys_values.shape[2]
    reach = 2 * latent
    packed = capacity * HEAD_DIM // 128
    cot = cotangent.reshape(regions, packed, 128)
    vmem = pl.BlockSpec(memory_space=pltpu.VMEM)
    hbm = pl.BlockSpec(memory_space=pl.ANY)
    dma = pltpu.SemaphoreType.DMA
    groups = regions // 8
    pair_grad, projection_grad = pl.pallas_call(
        functools.partial(kernel, regions, columns),
        name="region_backward",
        out_shape=(
            jax.ShapeDtypeStruct((2, HEAD_DIM, latent), F32),
            jax.ShapeDtypeStruct((HEAD_DIM, width), F32),
        ),
        in_specs=[pl.BlockSpec(memory_space=pltpu.SMEM), hbm, hbm, vmem, vmem],
        out_specs=(vmem, vmem),
        scratch_shapes=[
            pltpu.VMEM((regions, capacity, width), BF16),
            pltpu.VMEM((regions, packed, 128), BF16),
            pltpu.VMEM((2, HEAD_DIM, latent), BF16),
            pltpu.VMEM((reach, 2 * HEAD_DIM), BF16),
            pltpu.VMEM((2 * HEAD_DIM, reach), BF16),
            pltpu.VMEM((2 * HEAD_DIM, width), BF16),
            pltpu.VMEM((reach, 2 * HEAD_DIM), F32),
            pltpu.VMEM((HEAD_DIM, width), F32),
            [pltpu.VMEM((reach, 8 * capacity), F32)] * 2,
            [pltpu.VMEM((reach, 8 * capacity), BF16)] * 2,
            [pltpu.VMEM((8 * capacity, 2 * HEAD_DIM), BF16)] * 2,
            [pltpu.VMEM((8, 4 * capacity), F32)] * 2,
            pltpu.VMEM((2, HEAD_DIM, latent), BF16),
            pltpu.VMEM((2, HEAD_DIM, latent), BF16),
            pltpu.VMEM((8, 8, 128), F32),
            pltpu.VMEM((7, 8, 128), F32),
            pltpu.VMEM((groups, 8, 128), F32),
            pltpu.VMEM((8, 8, 128), F32),
            dma((regions,)),
            dma((regions,)),
            dma((regions // columns,)),
            dma((regions,)),
            dma,
            dma((1,)),
            dma((2,)),
            dma((2,)),
            dma((2, 7)),
            dma((2, groups)),
            dma((2, 8)),
        ],
        compiler_params=pltpu.CompilerParams(collective_id=0, has_side_effects=True),
    )(counts, observations[0], cot, keys_values, query_weight)
    return pl.pallas_call(
        hand_over,
        name="hand_over",
        out_shape=(
            jax.ShapeDtypeStruct(pair_grad.shape, F32),
            jax.ShapeDtypeStruct(projection_grad.shape, F32),
        ),
        in_specs=[vmem, vmem],
        out_specs=(vmem, vmem),
    )(pair_grad, projection_grad)


def solution(mesh):
    in_specs = (
        P("region", None, None, None),
        P("region", None, "mp", None),
        P(None, "mp", "region"),
        P("mp", None),
        P(),
    )
    out_specs = (P(None, "mp", "region"), P("mp", None))
    return jax.shard_map(
        per_device, mesh=mesh, in_specs=in_specs, out_specs=out_specs, check_vma=False
    )
```

```python
import functools
import math

import jax
import jax.numpy as jnp
from jax import lax
from jax.experimental import pallas as pl
from jax.experimental.pallas import tpu as pltpu
from jax.sharding import PartitionSpec as P

HEAD_DIM = 32
FIRST_LAG = 3
SECOND_LAG = 6
MESH = pl.DeviceIdType.MESH
F32 = jnp.float32
BF16 = jnp.bfloat16


def slot_of(source, here, chips):
    away = (source // 2 - here // 2 + chips) % chips
    half = away // (chips // 2)
    block = (away * (1 - half) + (chips - away) * half) % (chips // 2)
    return block * 4 + half * 2 + source % 2


def kernel(
    regions,
    columns,
    counts_hbm,
    obs_hbm,
    cot_hbm,
    kv_hbm,
    weight_hbm,
    pair_ref,
    proj_ref,
    counts_ref,
    kv_ref,
    weight_ref,
    obs_buf,
    cot_buf,
    kv_next,
    reach_rows,
    reach_cols,
    weight_rows,
    reach_acc,
    proj_acc,
    scores_buf,
    grads_buf,
    rows_buf,
    top_buf,
    edge_out,
    edge_in,
    part_out,
    part_in,
    group_in,
    final_in,
    obs_recv,
    cot_recv,
    obs_send,
    relay_send,
    cot_send,
    own_sems,
    kv_sems,
    edge_sems,
    part_sems,
    group_sems,
    final_sems,
):
    chips = regions // 2
    me = lax.axis_index("region")
    col = lax.axis_index("mp")
    my_chip = me // 2
    my_core = me % 2
    latent = kv_hbm.shape[2]
    blocks = regions // 4

    across = 4
    def along_x(i):
        return (col // across) * across + (col % across + i) % across

    def along_y(i):
        return (col + i * across) % columns

    barrier = pltpu.get_barrier_semaphore()

    def tell(sem, region, column):
        pl.semaphore_signal(sem, inc=1, device_id=(region, column), device_id_type=MESH)

    def greet_region(i, carry):
        offset = regions // 2 + (1 - 2 * (i % 2)) * ((i + 1) // 2)
        tell(barrier, (me + offset) % regions, col)
        return carry

    lax.fori_loop(0, regions - 1, greet_region, 0)
    for i in range(1, across):
        tell(barrier, me, along_x(i))
        tell(barrier, me, along_y(i))
    own_slot = my_core
    own_obs = pltpu.make_async_copy(obs_hbm.at[me], obs_buf.at[own_slot], obs_recv.at[own_slot])
    own_cot = pltpu.make_async_copy(cot_hbm.at[me], cot_buf.at[own_slot], cot_recv.at[own_slot])
    local = [
        pltpu.make_async_copy(counts_hbm, counts_ref, own_sems.at[0]),
        pltpu.make_async_copy(kv_hbm, kv_ref, own_sems.at[1]),
        pltpu.make_async_copy(weight_hbm, weight_ref, own_sems.at[2]),
    ]
    for copy in local:
        copy.start()
    own_obs.start()
    own_cot.start()

    pl.semaphore_wait(barrier, regions - 1 + 2 * (across - 1))
    kv_copy = pltpu.make_async_remote_copy(
        src_ref=kv_hbm,
        dst_ref=kv_next,
        send_sem=kv_sems.at[0],
        recv_sem=kv_sems.at[1],
        device_id=((me + regions - 1) % regions, col),
        device_id_type=MESH,
    )

    def obs_copy(peer):
        slot = slot_of(me, peer, chips)
        return pltpu.make_async_remote_copy(
            src_ref=obs_hbm.at[peer],
            dst_ref=obs_buf.at[slot],
            send_sem=obs_send.at[peer // columns],
            recv_sem=obs_recv.at[slot],
            device_id=(peer, col),
            device_id_type=MESH,
        )

    def cot_copy(chip, core, slot):
        peer = (chip % chips) * 2 + core
        return pltpu.make_async_remote_copy(
            src_ref=cot_hbm.at[peer],
            dst_ref=cot_buf.at[slot],
            send_sem=cot_send,
            recv_sem=cot_recv.at[slot],
            device_id=(peer, col),
            device_id_type=MESH,
        )

    kv_copy.start()
    def send_obs(share):
        peer = (me + (col - 2 * me + 2 * regions) % columns + columns * share) % regions

        @pl.when(peer != me)
        def _():
            obs_copy(peer).start()

    def send_at_distance(k, carry):
        for core in range(2):
            cot_copy(my_chip + k, core, k * 4 + 2 + my_core).start()
            cot_copy(my_chip + chips - k, core, k * 4 + my_core).start()
        return carry

    send_obs(0)
    send_obs(3)
    send_obs(1)
    send_obs(2)
    cot_copy(my_chip, 1 - my_core, my_core).start()
    lax.fori_loop(1, chips // 2, send_at_distance, 0)
    for core in range(2):
        cot_copy(my_chip + chips // 2, core, 2 + my_core).start()

    def wait_obs(slot):
        pltpu.make_async_copy(obs_hbm.at[0], obs_buf.at[slot], obs_recv.at[slot]).wait()

    def wait_cot(slot):
        pltpu.make_async_copy(cot_hbm.at[0], cot_buf.at[slot], cot_recv.at[slot]).wait()

    for copy in local:
        copy.wait()
    reach_cols[:HEAD_DIM, :latent] = kv_ref[0]
    reach_cols[HEAD_DIM:, :latent] = kv_ref[1]
    weight_rows[:HEAD_DIM] = weight_ref[...]
    weight_rows[HEAD_DIM:] = jnp.zeros_like(weight_ref)
    reach_acc[...] = jnp.zeros_like(reach_acc)
    proj_acc[...] = jnp.zeros_like(proj_acc)
    for ref in (*scores_buf, *grads_buf, *rows_buf, *top_buf):
        ref[...] = jnp.zeros_like(ref)
    kv_copy.wait_recv()
    reach_cols[:HEAD_DIM, latent:] = kv_next[0]
    reach_cols[HEAD_DIM:, latent:] = kv_next[1]
    reach_rows[...] = jnp.transpose(reach_cols[...].astype(F32)).astype(BF16)

    rows = 4 * obs_buf.shape[1]
    slots = obs_buf.shape[1]
    packed = cot_buf.shape[1]
    scale_back = 1.0 / math.sqrt(HEAD_DIM)
    power_scale = scale_back * math.log2(math.e)
    spread = (
        lax.broadcasted_iota(jnp.int32, (rows, 4 * packed), 0) // 4
        == lax.broadcasted_iota(jnp.int32, (rows, 4 * packed), 1)
    ).astype(F32).astype(BF16)

    fold = (
        lax.broadcasted_iota(jnp.int32, (4 * HEAD_DIM, 2 * HEAD_DIM), 0) % HEAD_DIM + HEAD_DIM
        == lax.broadcasted_iota(jnp.int32, (4 * HEAD_DIM, 2 * HEAD_DIM), 1)
    ).astype(F32).astype(BF16)
    row = lax.broadcasted_iota(jnp.int32, (slots, 4 * HEAD_DIM), 0)
    lane = lax.broadcasted_iota(jnp.int32, (slots, 4 * HEAD_DIM), 1)
    band = lane // HEAD_DIM == row % 4
    chunk = 128
    chunks = 2 * latent // chunk

    def source_at(block, part):
        half = part // 2
        away = jnp.where(block == 0, half * (chips // 2), jnp.where(half == 0, block, chips - block))
        return ((my_chip + away) % chips) * 2 + part % 2

    def relay(slot, peer):
        pltpu.make_async_remote_copy(
            src_ref=obs_buf.at[slot],
            dst_ref=obs_buf.at[slot],
            send_sem=relay_send.at[slot],
            recv_sem=obs_recv.at[slot],
            device_id=(me, peer),
            device_id_type=MESH,
        ).start()

    def in_line(part, owner):
        if part < 2:
            return owner // across == col // across
        return owner % across == col % across

    def each_part(block):
        for part in range(4):
            source = source_at(block, part)
            yield part, block * 4 + part, source, (source + me) % columns

    def spread_first(block):
        for part, slot, source, owner in each_part(block):

            @pl.when(jnp.logical_and(owner == col, source != me))
            def _():
                wait_obs(slot)
                for i in range(1, across):
                    relay(slot, along_x(i) if part < 2 else along_y(i))

    def spread_second(block):
        for part, slot, source, owner in each_part(block):

            @pl.when(jnp.logical_and(in_line(part, owner), source != me))
            def _():
                @pl.when(owner != col)
                def _():
                    wait_obs(slot)

                for i in range(1, across):
                    relay(slot, along_y(i) if part < 2 else along_x(i))

    def arrived(block):
        for part, slot, source, owner in each_part(block):
            wait_cot(slot)

            @pl.when(jnp.logical_or(jnp.logical_not(in_line(part, owner)), source == me))
            def _():
                wait_obs(slot)

    def block_obs(block):
        return obs_buf[pl.ds(block * 4, 4)].reshape(rows, obs_buf.shape[2])

    def fold_rows(value):
        return value.reshape(chunk // 8, 8, rows)

    def compute(block, last, even, front=True, middle=True):
        scores_now, scores_before = scores_buf[even], scores_buf[1 - even]
        grads_now, grads_before = grads_buf[1 - even], grads_buf[even]
        rows_ref = rows_buf[even]
        top = jnp.max(top_buf[1 - even][...], axis=0, keepdims=True)
        total = jnp.zeros((8, rows), F32)
        row_dot = jnp.zeros((8, rows), F32)
        query_grad = jnp.zeros((HEAD_DIM, rows), F32)
        for index in range(chunks):
            where = slice(index * chunk, (index + 1) * chunk)
            if middle:
                powers = jnp.exp2((scores_before[where, :rows] - top) * power_scale)
                scores_before[where, :rows] = powers
                total = total + jnp.sum(fold_rows(powers), axis=0)
                row_dot = row_dot + jnp.sum(fold_rows(powers * scores_before[where, rows:]), axis=0)
            reach_acc[where] += jnp.dot(
                grads_before[where], rows_ref[...], preferred_element_type=F32
            )
            if index % 2:
                pair = slice((index - 1) * chunk, (index + 1) * chunk)
                query_grad = query_grad + jnp.dot(
                    reach_cols[:HEAD_DIM, pair],
                    grads_before[pair, :rows],
                    preferred_element_type=F32,
                )
            if front and index == 1:
                cot = cot_buf[pl.ds(block * 4, 4)].reshape(4 * packed, cot_buf.shape[2])
                query = lax.dot_general(
                    block_obs(block),
                    weight_rows[...],
                    (((1,), (1,)), ((), ())),
                    preferred_element_type=F32,
                ).astype(BF16)
                wide = jnp.dot(spread, cot, preferred_element_type=F32)
                pieces = []
                for part in range(4):
                    live = counts_ref[source_at(block, part), me]
                    keep = jnp.logical_and(band, row < live)
                    pieces.append(jnp.where(keep, wide[part * slots : (part + 1) * slots], 0.0))
                wide = jnp.concatenate(pieces, axis=0).astype(BF16)
            if front and index == 4:
                grads = jnp.dot(wide, fold, preferred_element_type=F32).astype(BF16)
        if front:
            rows_ref[:rows] = query
            rows_ref[rows:] = grads
            both = jnp.concatenate([query, grads], axis=0)
        if middle:
            inverse = 1.0 / jnp.sum(total, axis=0, keepdims=True)
            row_dot = jnp.sum(row_dot, axis=0, keepdims=True) * inverse
        query_grad = (query_grad * scale_back).astype(BF16)
        highest = None
        for index in range(chunks):
            where = slice(index * chunk, (index + 1) * chunk)
            if front:
                products = lax.dot_general(
                    reach_rows[where], both, (((1,), (1,)), ((), ())), preferred_element_type=F32
                )
                scores_now[where] = products
                here = jnp.max(fold_rows(products[:, :rows]), axis=0)
                highest = here if highest is None else jnp.maximum(highest, here)
            if middle:
                attention = scores_before[where, :rows] * inverse
                score_grad = attention * (scores_before[where, rows:] - row_dot)
                grads_now[where, :rows] = score_grad.astype(BF16)
                grads_now[where, rows:] = attention.astype(BF16)
            if index == 3:
                proj_acc[...] += jnp.dot(query_grad, block_obs(last), preferred_element_type=F32)
        if front:
            top_buf[even][...] = highest

    def at(index):
        return (jnp.clip(index, 0, blocks - 1) + 1) % blocks

    def stage(step, even):
        @pl.when(step < blocks)
        def _():
            spread_first((step + 1) % blocks)

        @pl.when(jnp.logical_and(step >= FIRST_LAG, step < blocks + FIRST_LAG))
        def _():
            spread_second((step - FIRST_LAG + 1) % blocks)

        index = step - SECOND_LAG

        @pl.when(jnp.logical_and(index >= 0, index < blocks))
        def _():
            arrived(at(index))

        @pl.when(index >= 0)
        def _():
            compute(at(index), at(index - 2), even)

    def stages(pair, carry):
        for even in range(2):
            stage(pair * 2 + even, even)
        return carry

    lax.fori_loop(0, (blocks + SECOND_LAG) // 2, stages, 0)
    compute(0, at(blocks - 2), 0, front=False)
    compute(0, at(blocks - 1), 1, front=False, middle=False)

    group = me // 8
    member = me % 8
    groups = regions // 8
    tiles = [(r, c) for r in range(0, proj_acc.shape[0], 8) for c in range(0, proj_acc.shape[1], 128)]
    for index, (r, c) in enumerate(tiles):
        part_out[index] = proj_acc[r : r + 8, c : c + 128]

    def part_copy(i):
        peer = (member + i) % 8
        return pltpu.make_async_remote_copy(
            src_ref=part_out.at[peer],
            dst_ref=part_in.at[i - 1],
            send_sem=part_sems.at[0, i - 1],
            recv_sem=part_sems.at[1, i - 1],
            device_id=(group * 8 + peer, col),
            device_id_type=MESH,
        )

    for i in range(1, 8):
        part_copy(i).start()

    reach_grad = jnp.transpose(reach_acc[...])
    key_grad = reach_grad[:HEAD_DIM] * scale_back
    value_grad = reach_grad[HEAD_DIM:]
    edge_out[0] = key_grad[:, latent:].astype(BF16)
    edge_out[1] = value_grad[:, latent:].astype(BF16)
    edge_copy = pltpu.make_async_remote_copy(
        src_ref=edge_out,
        dst_ref=edge_in,
        send_sem=edge_sems.at[0],
        recv_sem=edge_sems.at[1],
        device_id=((me + 1) % regions, col),
        device_id_type=MESH,
    )
    edge_copy.start()
    pair_ref[0] = key_grad[:, :latent]
    pair_ref[1] = value_grad[:, :latent]

    for i in range(1, 8):
        part_copy(i).wait_recv()
    total = part_out[member]
    for i in range(1, 8):
        total = total + part_in[i - 1]
    group_in[group] = total

    def group_copy(i):
        peer = (group + i) % groups
        return pltpu.make_async_remote_copy(
            src_ref=group_in.at[group],
            dst_ref=group_in.at[group],
            send_sem=group_sems.at[0, i - 1],
            recv_sem=group_sems.at[1, group],
            device_id=(peer * 8 + member, col),
            device_id_type=MESH,
        )

    for i in sorted(range(1, groups), key=lambda i: -min(i, groups - i)):
        group_copy(i).start()

    def sent_block(block, carry):
        for part, slot, source, owner in each_part(block):

            @pl.when(jnp.logical_and(owner == col, source != me))
            def _():
                obs_copy(source).wait_send()
                many = pl.ds(0, 2 * across - 2)
                pltpu.make_async_copy(obs_buf.at[many], obs_buf.at[many], relay_send.at[slot]).wait()

            @pl.when(
                jnp.logical_and(
                    jnp.logical_and(in_line(part, owner), owner != col), source != me
                )
            )
            def _():
                many = pl.ds(0, across - 1)
                pltpu.make_async_copy(obs_buf.at[many], obs_buf.at[many], relay_send.at[slot]).wait()

        return carry

    lax.fori_loop(0, blocks, sent_block, 0)
    edge_copy.wait_recv()
    pair_ref[...] += edge_in[...].astype(F32)

    for i in range(1, groups):
        peer = (group + i) % groups
        pltpu.make_async_copy(
            group_in.at[peer], group_in.at[peer], group_sems.at[1, peer]
        ).wait()
    total = group_in[0]
    for index in range(1, groups):
        total = total + group_in[index]
    final_in[member] = total * (1.0 / regions)

    def final_copy(i):
        peer = (member + i) % 8
        return pltpu.make_async_remote_copy(
            src_ref=final_in.at[member],
            dst_ref=final_in.at[member],
            send_sem=final_sems.at[0, i - 1],
            recv_sem=final_sems.at[1, member],
            device_id=(group * 8 + peer, col),
            device_id_type=MESH,
        )

    for i in range(1, 8):
        final_copy(i).start()
    for i in range(1, 8):
        peer = (member + i) % 8
        pltpu.make_async_copy(
            final_in.at[peer], final_in.at[peer], final_sems.at[1, peer]
        ).wait()
    for index, (r, c) in enumerate(tiles):
        proj_ref[r : r + 8, c : c + 128] = final_in[index]

    kv_copy.wait_send()
    edge_copy.wait_send()
    many = pl.ds(0, regions - 1)
    pltpu.make_async_copy(cot_buf.at[many], cot_buf.at[many], cot_send).wait()
    for i in range(1, 8):
        part_copy(i).wait_send()
        final_copy(i).wait_send()
    for i in range(1, groups):
        group_copy(i).wait_send()


def hand_over(pair_in, proj_in, pair_out, proj_out):
    pair_out[...] = pair_in[...]
    proj_out[...] = proj_in[...]


def per_device(observations, cotangent, keys_values, query_weight, counts):
    regions = lax.axis_size("region")
    columns = lax.axis_size("mp")
    capacity = observations.shape[2]
    width = observations.shape[3]
    latent = keys_values.shape[2]
    reach = 2 * latent
    packed = capacity * HEAD_DIM // 128
    cot = cotangent.reshape(regions, packed, 128)
    vmem = pl.BlockSpec(memory_space=pltpu.VMEM)
    hbm = pl.BlockSpec(memory_space=pl.ANY)
    dma = pltpu.SemaphoreType.DMA
    groups = regions // 8
    pair_grad, projection_grad = pl.pallas_call(
        functools.partial(kernel, regions, columns),
        name="region_backward",
        out_shape=(
            jax.ShapeDtypeStruct((2, HEAD_DIM, latent), F32),
            jax.ShapeDtypeStruct((HEAD_DIM, width), F32),
        ),
        in_specs=[hbm] * 5,
        out_specs=(vmem, vmem),
        scratch_shapes=[
            pltpu.SMEM(counts.shape, jnp.int32),
            pltpu.VMEM((2, HEAD_DIM, latent), BF16),
            pltpu.VMEM((HEAD_DIM, width), BF16),
            pltpu.VMEM((regions, capacity, width), BF16),
            pltpu.VMEM((regions, packed, 128), BF16),
            pltpu.VMEM((2, HEAD_DIM, latent), BF16),
            pltpu.VMEM((reach, 2 * HEAD_DIM), BF16),
            pltpu.VMEM((2 * HEAD_DIM, reach), BF16),
            pltpu.VMEM((2 * HEAD_DIM, width), BF16),
            pltpu.VMEM((reach, 2 * HEAD_DIM), F32),
            pltpu.VMEM((HEAD_DIM, width), F32),
            [pltpu.VMEM((reach, 8 * capacity), F32)] * 2,
            [pltpu.VMEM((reach, 8 * capacity), BF16)] * 2,
            [pltpu.VMEM((8 * capacity, 2 * HEAD_DIM), BF16)] * 2,
            [pltpu.VMEM((8, 4 * capacity), F32)] * 2,
            pltpu.VMEM((2, HEAD_DIM, latent), BF16),
            pltpu.VMEM((2, HEAD_DIM, latent), BF16),
            pltpu.VMEM((8, 8, 128), F32),
            pltpu.VMEM((7, 8, 128), F32),
            pltpu.VMEM((groups, 8, 128), F32),
            pltpu.VMEM((8, 8, 128), F32),
            dma((regions,)),
            dma((regions,)),
            dma((regions // columns,)),
            dma((regions,)),
            dma,
            dma((3,)),
            dma((2,)),
            dma((2,)),
            dma((2, 7)),
            dma((2, groups)),
            dma((2, 8)),
        ],
        compiler_params=pltpu.CompilerParams(collective_id=0, has_side_effects=True),
    )(counts, observations[0], cot, keys_values, query_weight)
    return pl.pallas_call(
        hand_over,
        name="hand_over",
        out_shape=(
            jax.ShapeDtypeStruct(pair_grad.shape, F32),
            jax.ShapeDtypeStruct(projection_grad.shape, F32),
        ),
        in_specs=[vmem, vmem],
        out_specs=(vmem, vmem),
    )(pair_grad, projection_grad)


def solution(mesh):
    in_specs = (
        P("region", None, None, None),
        P("region", None, "mp", None),
        P(None, "mp", "region"),
        P("mp", None),
        P(),
    )
    out_specs = (P(None, "mp", "region"), P("mp", None))
    return jax.shard_map(
        per_device, mesh=mesh, in_specs=in_specs, out_specs=out_specs, check_vma=False
    )
```
